32 devices in a mesh: ctx: 8 (over z, y), head: 4 (over x, core).
Axes of the slice: x: 2, y: 2, z: 4, core: 2. Of those that a mesh axis runs over, the one named last changes fastest.
Arguments:
- queries: bfloat16 [1024, 4096], P('ctx', 'head'), may hold values from -0.75 to 0.75
- keys: bfloat16 [1024, 4096], P('ctx', 'head'), may hold values from -0.75 to 0.75
- values: bfloat16 [1024, 4096], P('ctx', 'head'), may hold values from -0.75 to 0.75
- out_grad: bfloat16 [1024, 4096], P('ctx', 'head'), may hold values from -0.75 to 0.75
- log_decay: float32 [32, 1024], P('head', 'ctx'), may hold values from -1.5 to 0, as said below
- prefix_state: float32 [32, 128, 128], P('head'), may hold values from -3 to 3
- moe_input: bfloat16 [1024, 3072], P('ctx', 'head'), may hold values from -6 to 6
- moe_grad: bfloat16 [1024, 3072], P('ctx', 'head'), may hold values from -6 to 6
- expert_gate: bfloat16 [8, 3072, 4608], P('ctx', None, 'head'), may hold values from -0.109375 to 0.109375
- expert_up: bfloat16 [8, 3072, 4608], P('ctx', None, 'head'), may hold values from -0.109375 to 0.109375
- expert_down: bfloat16 [8, 4608, 3072], P('ctx', 'head'), may hold values from -0.09375 to 0.09375
- expert_ids: int32 [1024, 2], P('ctx'), may hold values from 0 to 7, all different within a row; in each aligned block of 128 rows (0 to 127, 128 to 255, ...) at most 64 rows name the same one
- route_probs: float32 [1024, 2], P('ctx'), may hold values from 0.1 to 1
Outputs:
- query_grad: bfloat16 [1024, 4096], P('ctx', 'head')
- key_grad: bfloat16 [1024, 4096], P('ctx', 'head')
- value_grad: bfloat16 [1024, 4096], P('ctx', 'head')
- moe_input_grad: bfloat16 [1024, 3072], P('ctx', 'head')
The draws below stay inside these ranges and needn't reach their ends.
Inputs may be any that keep to these rules, and one draw needn't show every extreme that they name: `expert_ids`: each row names two different experts. In each block of 128 rows (one ctx index) no expert is named by more than 64 rows, and in every draw some expert is named by exactly 64 rows of some block. `log_decay`: log of the factor by which a head's state is multiplied at a position.
All inputs are finite; a program needn't handle non-finite values.
Results may differ from the reference program's by a relative error of at most 0.019.
Values may be sent and summed in bfloat16 or wider, within the bound.
No kernel may reach another device: no remote copies, remote signals or barrier semaphores. Data moves between devices by JAX's collectives and lax.ppermute only.
A program may use at most 128 MiB of HBM per device.

```python
import math
import jax
import jax.numpy as jnp
import numpy as np
from jax import lax

D = 3072
FF = 4608
HEAD_COUNT = 32
HDIM = 128
TOK_DEV = 128
WINDOW_TOKENS = 1024
EXPERTS = 8
CAP = 64
N_CTX = 8
N_HEAD = 4


def draw_log_decay(key, part):
    random_keys_split = jax.random.split(jax.random.fold_in(key, 11), 6)
    fast_share = 0.5
    is_fast = jax.random.uniform(random_keys_split[0], (HEAD_COUNT,)) < fast_share
    fast_rate = jax.random.uniform(random_keys_split[1], (HEAD_COUNT,), minval=1.0 / 50.0, maxval=1.0 / 30.0)
    base_rate = jnp.where(is_fast, fast_rate, 0.3 / WINDOW_TOKENS)
    blocks = WINDOW_TOKENS // TOK_DEV
    block_factor = jnp.exp(jax.random.uniform(random_keys_split[2], (HEAD_COUNT, blocks), minval=-0.6931, maxval=0.6931))
    block_factor = jnp.repeat(block_factor, TOK_DEV, axis=1)
    position_factor = jax.random.uniform(random_keys_split[3], (HEAD_COUNT, WINDOW_TOKENS), minval=0.6, maxval=1.4)
    decay_rate = base_rate[:, None] * block_factor * position_factor
    spike_location = jax.random.randint(random_keys_split[4], (HEAD_COUNT, 2), 0, WINDOW_TOKENS)
    spike_retained = jax.random.uniform(random_keys_split[5], (HEAD_COUNT, 2), minval=0.5, maxval=0.8)
    token_positions = jnp.arange(WINDOW_TOKENS, dtype=jnp.int32)
    spike_events = jnp.sum(jnp.where(token_positions[None, None, :] == spike_location[:, :, None], jnp.log(spike_retained)[:, :, None], 0.0), axis=1)
    return (spike_events - decay_rate).astype(jnp.float32)


def block_levels(own_key, shape, pieces, low, largest):
    factor_of = 1.0
    for dim, blocks in pieces:
        draws = jax.random.uniform(jax.random.fold_in(jax.random.fold_in(own_key, 6), dim), (blocks,), jnp.float32, low / len(pieces), largest / len(pieces))
        factor_of = factor_of * jnp.repeat(jnp.exp(draws), shape[dim] // blocks).reshape((-1,) + (1,) * (len(shape) - 1 - dim))
    return factor_of


def deal_out(key, own, number, rows, count, top, reach, lean):
    order = jax.random.permutation(key, count)
    packed, usual = shares(count, rows * top, reach, lean, True), shares(count, rows * top, reach, lean, False)
    places = jnp.arange(count)

    def named(tallies, turn):
        used = int((tallies > 0).sum())
        fixed = max(1, used // 4)
        moved = fixed + (places - fixed + turn * (used - fixed)) % max(1, count - fixed)
        return jnp.zeros((count,), jnp.int32).at[order[jnp.where(places < fixed, places, moved)]].set(jnp.asarray(tallies, jnp.int32))

    tallies = jnp.where(number % 4 == 0, named(packed, number // 4), named(usual, number - number // 4 - 1))
    mixed = jax.random.permutation(jax.random.fold_in(own, 3), count)
    source_of, receiver = mixed[0:count // 2 * 2:2], mixed[1:count // 2 * 2:2]
    room = jnp.minimum(tallies[source_of] - 1, reach - tallies[receiver]) // 2
    room = jnp.where((source_of == order[0]) | (receiver == order[0]) | (tallies[receiver] == 0), 0, jnp.maximum(room, 0))
    moved = jax.random.randint(jax.random.fold_in(own, 4), (count // 2,), 0, 1 << 20) % (room + 1)
    tallies = tallies.at[source_of].add(-moved).at[receiver].add(moved)
    items = jnp.searchsorted(jnp.cumsum(tallies), jnp.arange(rows * top), side="right").astype(jnp.int32)
    table = items.reshape(top, rows).T
    table = table[jax.random.permutation(jax.random.fold_in(own, 1), rows)]
    turn = jax.random.randint(jax.random.fold_in(own, 2), (rows, 1), 0, top)
    return jnp.take_along_axis(table, (jnp.arange(top)[None, :] + turn) % top, axis=1)


def shares(count, total, bound, slope, full):
    portions = [(1 << 20) // math.isqrt(grade ** slope) + 1 for grade in range(1, count + 1)]
    largest = bound if full else min(bound, max(-(-total // count), total * portions[0] // sum(portions)))
    least = 1 if total - largest >= count - 1 else 0
    holding, surplus = [largest] + [least] * (count - 1), total - largest - least * (count - 1)
    while surplus > 0:
        free = [i for i in range(1, count) if holding[i] < largest] or [i for i in range(1, count) if holding[i] < bound]
        pool, left = sum([portions[i] for i in free]), surplus
        for i in free:
            extra = min(bound - holding[i], max(1, left * portions[i] // pool), surplus)
            holding[i] = holding[i] + extra
            surplus = surplus - extra
    return np.array(holding)


def bell_draw(own_key, shape, width, limit, cuts=(), held_as=jnp.bfloat16):
    values = width * jax.random.normal(own_key, shape, jnp.float32)
    if cuts:
        values = values * block_levels(own_key, shape, cuts, -0.22, 0.18)
    return jnp.clip(values, -limit, limit).astype(held_as)


def setup_inputs(seed: int = 0) -> dict:
    key_of = jax.random.split(jax.random.key(seed), 14)
    queries = bell_draw(key_of[0], (WINDOW_TOKENS, HEAD_COUNT * HDIM), 0.125, 0.75, ((0, 8), (1, 4)))
    keys = bell_draw(key_of[1], (WINDOW_TOKENS, HEAD_COUNT * HDIM), 0.125, 0.75, ((0, 8), (1, 4)))
    values = bell_draw(key_of[2], (WINDOW_TOKENS, HEAD_COUNT * HDIM), 0.125, 0.75, ((0, 8), (1, 4)))
    out_grad = bell_draw(key_of[3], (WINDOW_TOKENS, HEAD_COUNT * HDIM), 0.125, 0.75, ((0, 8), (1, 4)))
    log_decay = draw_log_decay(jax.random.fold_in(key_of[13], 71), 0)
    prefix_state = bell_draw(key_of[5], (HEAD_COUNT, HDIM, HDIM), 0.5, 3.0, ((0, 4),), jnp.float32)
    moe_input = bell_draw(key_of[6], (WINDOW_TOKENS, D), 1.0, 6.0, ((0, 8), (1, 4)))
    moe_grad = bell_draw(key_of[7], (WINDOW_TOKENS, D), 1.0, 6.0, ((0, 8), (1, 4)))
    expert_gate = bell_draw(key_of[8], (EXPERTS, D, FF), D ** -0.5, 0.109375, ((0, 8), (2, 4)))
    expert_up = bell_draw(key_of[9], (EXPERTS, D, FF), D ** -0.5, 0.109375, ((0, 8), (2, 4)))
    expert_down = bell_draw(key_of[10], (EXPERTS, FF, D), FF ** -0.5, 0.09375, ((0, 8), (1, 4)))
    expert_ids_keys = jax.random.split(jax.random.fold_in(key_of[11], 1), WINDOW_TOKENS // TOK_DEV)
    expert_ids_turns = jax.random.permutation(jax.random.fold_in(key_of[11], 3), WINDOW_TOKENS // TOK_DEV)
    expert_ids = jax.vmap(lambda own, number: deal_out(jax.random.fold_in(key_of[11], 2), own, number, TOK_DEV, EXPERTS, 2, CAP, 2))(expert_ids_keys, expert_ids_turns).reshape((WINDOW_TOKENS, 2))
    route_probs = jnp.clip(0.1 + 0.9 * jax.random.uniform(key_of[12], (WINDOW_TOKENS, 2), jnp.float32) ** block_levels(key_of[12], (WINDOW_TOKENS, 2), ((0, 8),), -0.2, 0.2), 0.1, 1.0)
    return dict(queries=queries, keys=keys, values=values, out_grad=out_grad, log_decay=log_decay, prefix_state=prefix_state, moe_input=moe_input, moe_grad=moe_grad, expert_gate=expert_gate, expert_up=expert_up, expert_down=expert_down, expert_ids=expert_ids, route_probs=route_probs)


HIGHEST = lax.Precision.HIGHEST


def decay_factors(log_decay):
    cumulative = jnp.cumsum(log_decay, axis=1)
    totals = cumulative[:, -1]
    token_positions = jnp.arange(log_decay.shape[1], dtype=jnp.int32)
    causal = (token_positions[:, None] >= token_positions[None, :])[None]
    spread = cumulative[:, :, None] - cumulative[:, None, :]
    within = jnp.where(causal, jnp.exp(jnp.where(causal, spread, 0.0)), 0.0)
    tail_decay = jnp.exp(totals[:, None] - cumulative)
    front_decay = jnp.exp(cumulative)
    return totals, within, tail_decay, front_decay


def block_summaries(query_heads, key_heads, value_heads, grad_heads, tail_decay, front_decay):
    key_state = jnp.einsum('hsi,hsj->hij', key_heads * tail_decay[:, :, None], value_heads, precision=HIGHEST)
    query_state = jnp.einsum('hti,htj->hij', query_heads * front_decay[:, :, None], grad_heads, precision=HIGHEST)
    return key_state, query_state


def block_grads(query_heads, key_heads, value_heads, grad_heads, within, tail_decay, front_decay, state_in, state_grad):
    value_scores = jnp.einsum('hti,hsi->hts', grad_heads, value_heads, precision=HIGHEST) * within
    key_scores = jnp.einsum('hti,hsi->hts', query_heads, key_heads, precision=HIGHEST) * within
    query_out = jnp.einsum('hts,hsi->hti', value_scores, key_heads, precision=HIGHEST)
    query_out = query_out + front_decay[:, :, None] * jnp.einsum('htj,hij->hti', grad_heads, state_in, precision=HIGHEST)
    key_out = jnp.einsum('hts,hti->hsi', value_scores, query_heads, precision=HIGHEST)
    key_out = key_out + tail_decay[:, :, None] * jnp.einsum('hsj,hij->hsi', value_heads, state_grad, precision=HIGHEST)
    value_out = jnp.einsum('hts,htj->hsj', key_scores, grad_heads, precision=HIGHEST)
    value_out = value_out + tail_decay[:, :, None] * jnp.einsum('hsi,hij->hsj', key_heads, state_grad, precision=HIGHEST)
    return query_out, key_out, value_out


def swiglu_grads(gate_pre, up_pre, hidden_grad):
    sigmoid = jax.nn.sigmoid(gate_pre)
    gate_grad = hidden_grad * up_pre * sigmoid * (1.0 + gate_pre * (1.0 - sigmoid))
    up_grad = hidden_grad * gate_pre * sigmoid
    return gate_grad.astype(jnp.bfloat16), up_grad.astype(jnp.bfloat16)


def block_slots(block_ids, experts, capacity):
    flat_ids = block_ids.reshape(-1)
    onehot = (flat_ids[:, None] == jnp.arange(experts, dtype=jnp.int32)[None, :]).astype(jnp.int32)
    earlier = jnp.cumsum(onehot, axis=0) - onehot
    slot_rank = jnp.sum(earlier * onehot, axis=1).astype(jnp.int32)
    placed = (flat_ids * capacity + slot_rank).astype(jnp.int32)
    pair_index = jnp.arange(flat_ids.shape[0], dtype=jnp.int32)
    source = jnp.zeros((experts * capacity,), jnp.int32).at[placed].set(pair_index // 2)
    filled = jnp.zeros((experts * capacity,), jnp.float32).at[placed].set(1.0)
    return placed, source, filled


def split_heads(array):
    return array.astype(jnp.float32).reshape(N_CTX, TOK_DEV, HEAD_COUNT, HDIM).transpose(0, 2, 1, 3)


def join_heads(array):
    return array.transpose(0, 2, 1, 3).reshape(WINDOW_TOKENS, HEAD_COUNT * HDIM).astype(jnp.bfloat16)


def reference(queries, keys, values, out_grad, log_decay, prefix_state, moe_input, moe_grad, expert_gate, expert_up, expert_down, expert_ids, route_probs):
    query_blocks = split_heads(queries)
    key_blocks = split_heads(keys)
    value_blocks = split_heads(values)
    grad_blocks = split_heads(out_grad)
    decay_blocks = log_decay.reshape(HEAD_COUNT, N_CTX, TOK_DEV).transpose(1, 0, 2)

    def summarize(items):
        query_heads, key_heads, value_heads, grad_heads, decays = items
        totals, within, tail_decay, front_decay = decay_factors(decays)
        key_state, query_state = block_summaries(query_heads, key_heads, value_heads, grad_heads, tail_decay, front_decay)
        return totals, key_state, query_state

    totals, key_states, query_states = lax.map(summarize, (query_blocks, key_blocks, value_blocks, grad_blocks, decay_blocks))

    def forward(carried, items):
        block_total, key_state = items
        return jnp.exp(block_total)[:, None, None] * carried + key_state, carried

    final_state, states_in = lax.scan(forward, prefix_state, (totals, key_states))

    def backward(carried, items):
        block_total, query_state = items
        return query_state + jnp.exp(block_total)[:, None, None] * carried, carried

    first_grad, states_grad = lax.scan(backward, jnp.zeros_like(prefix_state), (totals, query_states), reverse=True)

    def finish(items):
        query_heads, key_heads, value_heads, grad_heads, decays, state_in, state_grad = items
        block_total, within, tail_decay, front_decay = decay_factors(decays)
        return block_grads(query_heads, key_heads, value_heads, grad_heads, within, tail_decay, front_decay, state_in, state_grad)

    query_out, key_out, value_out = lax.map(finish, (query_blocks, key_blocks, value_blocks, grad_blocks, decay_blocks, states_in, states_grad))

    experts = N_CTX
    capacity = CAP
    placed, source, filled = jax.vmap(lambda block_ids: block_slots(block_ids, experts, capacity))(expert_ids.reshape(N_CTX, TOK_DEV, 2))
    global_source = source + (jnp.arange(N_CTX, dtype=jnp.int32) * TOK_DEV)[:, None]
    rows_source = global_source.reshape(N_CTX, experts, capacity).transpose(1, 0, 2).reshape(experts, N_CTX * capacity)
    rows_filled = filled.reshape(N_CTX, experts, capacity).transpose(1, 0, 2).reshape(experts, N_CTX * capacity)
    span = FF // N_HEAD

    def one_expert(items):
        index, present, gate_w, up_w, down_w = items
        rows_in = (moe_input[index].astype(jnp.float32) * present[:, None]).astype(jnp.bfloat16)
        rows_grad = (moe_grad[index].astype(jnp.float32) * present[:, None]).astype(jnp.bfloat16)
        gate_pre = jnp.dot(rows_in, gate_w, preferred_element_type=jnp.float32)
        up_pre = jnp.dot(rows_in, up_w, preferred_element_type=jnp.float32)
        hidden_grad = jnp.dot(rows_grad, down_w.T, preferred_element_type=jnp.float32)
        gate_grad, up_grad = swiglu_grads(gate_pre, up_pre, hidden_grad)
        gate_parts = gate_grad.astype(jnp.float32).reshape(-1, N_HEAD, span)
        up_parts = up_grad.astype(jnp.float32).reshape(-1, N_HEAD, span)
        parts = jnp.einsum('nhf,dhf->hnd', gate_parts, gate_w.astype(jnp.float32).reshape(D, N_HEAD, span))
        parts = parts + jnp.einsum('nhf,dhf->hnd', up_parts, up_w.astype(jnp.float32).reshape(D, N_HEAD, span))
        parts = lax.optimization_barrier(parts.astype(jnp.bfloat16))
        return jnp.sum(parts.astype(jnp.float32), axis=0).astype(jnp.bfloat16)

    expert_back = lax.map(one_expert, (rows_source, rows_filled, expert_gate, expert_up, expert_down))
    table = expert_back.reshape(experts * N_CTX * capacity, D)
    pair_ids = expert_ids.reshape(N_CTX, TOK_DEV * 2)
    slot_rank = placed - pair_ids * capacity
    rows_index = pair_ids * (N_CTX * capacity) + (jnp.arange(N_CTX, dtype=jnp.int32) * capacity)[:, None] + slot_rank
    picked = table[rows_index.reshape(-1)].astype(jnp.float32).reshape(WINDOW_TOKENS, 2, D)
    moe_input_grad = jnp.sum(picked * route_probs[:, :, None], axis=1).astype(jnp.bfloat16)
    return join_heads(query_out), join_heads(key_out), join_heads(value_out), moe_input_grad
```

```python
import functools

import jax
import jax.numpy as jnp
from jax import lax
from jax.experimental import pallas as pl
from jax.experimental.pallas import tpu as pltpu
from jax.sharding import PartitionSpec as P

F32 = jnp.float32
BF16 = jnp.bfloat16
HIGHEST = lax.Precision.HIGHEST
NT = (((1,), (1,)), ((), ()))
TN = (((0,), (0,)), ((), ()))
NN = (((1,), (0,)), ((), ()))
ANY = pl.BlockSpec(memory_space=pl.ANY)
SMEM = pl.BlockSpec(memory_space=pltpu.SMEM)


def dot(a, b, dims=NN, precision=None):
    return lax.dot_general(a, b, dims, precision=precision, preferred_element_type=F32)


def xor_permute(array, axis, mask):
    size = lax.axis_size(axis)
    return lax.ppermute(array, axis, [(i, i ^ mask) for i in range(size)])


def cost(flops, moved):
    return pl.CostEstimate(flops=int(flops), bytes_accessed=int(moved), transcendentals=0)


def route_kernel(n, cap, ctx_ref, ids_ref, ids_t_ref, probs_ref, *refs):
    x_refs, (w_hi_ref, w_lo_ref), out_refs = refs[:2], refs[2:4], refs[4:]
    me = ctx_ref[0]
    tokens = ids_ref.shape[0]
    rows = n * cap
    shift = cap.bit_length() - 1
    before = lax.broadcasted_iota(jnp.int32, (tokens, tokens), 0)
    after = lax.broadcasted_iota(jnp.int32, (tokens, tokens), 1)

    place = lax.broadcasted_iota(jnp.int32, (rows, tokens), 0)
    rel = place >> shift
    named = ((ids_t_ref[0:1, :] ^ me) == rel) | ((ids_t_ref[1:2, :] ^ me) == rel)
    earlier = dot(named.astype(F32).astype(BF16), (before < after).astype(F32).astype(BF16))
    chosen = named & (earlier.astype(jnp.int32) == (place & (cap - 1)))
    pick = chosen.astype(F32).astype(BF16)
    for x_ref, even_ref, odd_ref in zip(x_refs, out_refs[0::2], out_refs[1::2]):
        got = dot(pick, x_ref[...]).astype(BF16)
        for m in range(n // 2):
            even_ref[m] = got[2 * m * cap : (2 * m + 1) * cap]
            odd_ref[m] = got[(2 * m + 1) * cap : (2 * m + 2) * cap]

    lane = lax.broadcasted_iota(jnp.int32, (tokens, rows), 1)
    rel = lane >> shift
    first = (ids_ref[:, 0:1] ^ me) == rel
    second = (ids_ref[:, 1:2] ^ me) == rel
    named = first | second
    earlier = dot((after < before).astype(F32).astype(BF16), named.astype(F32).astype(BF16))
    chosen = named & (earlier.astype(jnp.int32) == (lane & (cap - 1)))
    weight = jnp.where(first, probs_ref[:, 0:1], probs_ref[:, 1:2])
    weight = jnp.where(chosen, weight, 0.0)
    high = weight.astype(BF16)
    w_hi_ref[...] = high
    w_lo_ref[...] = (weight - high.astype(F32)).astype(BF16)


def route(ctx, ids, probs, x_in, x_grad, n, cap):
    tokens, width = x_in.shape
    half = jax.ShapeDtypeStruct((n // 2, cap, width), BF16)
    weight = jax.ShapeDtypeStruct((tokens, n * cap), BF16)
    return pl.pallas_call(
        functools.partial(route_kernel, n, cap),
        name="route",
        out_shape=[weight, weight, half, half, half, half],
        in_specs=[SMEM] + [pl.BlockSpec(memory_space=pltpu.VMEM)] * 5,
        cost_estimate=cost(4 * n * cap * tokens * width, 8 * n * cap * width),
    )(ctx, ids, ids.T, probs, x_in, x_grad)


def fetch_pieces(piece_refs, buffer, sems, parts):
    rows = piece_refs[0].shape[0]
    copies = []
    for i, ref in enumerate(piece_refs):
        k, p = i // parts, i % parts
        copies.append(
            pltpu.make_async_copy(ref, buffer.at[k, pl.ds(p * rows, rows)], sems.at[k, p])
        )
    return copies


def await_pieces(piece_refs, buffer, sems, parts, step):
    rows = piece_refs[0].shape[0]
    for p in range(parts):
        pltpu.make_async_copy(
            piece_refs[p], buffer.at[step, pl.ds(p * rows, rows)], sems.at[step, p]
        ).wait()


def gate_up_kernel(steps, parts, blk_ref, *refs):
    pieces = refs[: steps * parts]
    gate_ref, up_ref, a_ref, b_ref, buffer, gate_acc, up_acc, sems = refs[steps * parts :]
    j = pl.program_id(0)

    @pl.when(j == 0)
    def _():
        for copy in fetch_pieces(pieces, buffer, sems, parts):
            copy.start()

    await_pieces(pieces, buffer, sems, parts, j)
    x = buffer[j]
    gate = dot(x, gate_ref[...])
    up = dot(x, up_ref[...])

    @pl.when(j == 0)
    def _():
        gate_acc[...] = gate
        up_acc[...] = up

    @pl.when((j > 0) & (j < steps - 1))
    def _():
        gate_acc[...] += gate
        up_acc[...] += up

    @pl.when(j == steps - 1)
    def _():
        g = gate_acc[...] + gate
        u = up_acc[...] + up
        sig = jax.nn.sigmoid(g)
        a_ref[...] = (u * sig * (1.0 + g * (1.0 - sig))).astype(BF16)
        b_ref[...] = (g * sig).astype(BF16)


def gate_up(blocks, pieces, gate, up, steps, parts):
    rows = pieces[0].shape[0] * parts
    depth = pieces[0].shape[1]
    hidden = gate.shape[2]
    weight = pl.BlockSpec((None, depth, hidden), lambda j, blk: (0, blk[j], 0))
    out = pl.BlockSpec((rows, hidden), lambda j, blk: (0, 0))
    return pl.pallas_call(
        functools.partial(gate_up_kernel, steps, parts),
        name="gate_up",
        grid_spec=pltpu.PrefetchScalarGridSpec(
            num_scalar_prefetch=1,
            grid=(steps,),
            in_specs=[ANY] * len(pieces) + [weight, weight],
            out_specs=[out, out],
            scratch_shapes=[
                pltpu.VMEM((steps, rows, depth), BF16),
                pltpu.VMEM((rows, hidden), F32),
                pltpu.VMEM((rows, hidden), F32),
                pltpu.SemaphoreType.DMA((steps, parts)),
            ],
        ),
        out_shape=[jax.ShapeDtypeStruct((rows, hidden), BF16)] * 2,
        cost_estimate=cost(4 * rows * depth * steps * hidden, 4 * depth * steps * hidden),
    )(blocks, *pieces, gate, up)


def hidden_kernel(steps, parts, blk_ref, *refs):
    pieces = refs[: steps * parts]
    (down_ref, gate_hbm, up_hbm, a_ref, b_ref, gg_ref, ug_ref, out_a, out_b) = refs[
        steps * parts : steps * parts + 9
    ]
    buffer, acc, gate_w, up_w, sems, wsems = refs[steps * parts + 9 :]
    j = pl.program_id(0)
    depth = gate_w.shape[1]

    def weights(i):
        block = blk_ref[steps + i]
        span = pl.ds(pl.multiple_of(block * depth, depth), depth)
        return (
            pltpu.make_async_copy(gate_hbm.at[0, span], gate_w.at[i], wsems.at[i, 0]),
            pltpu.make_async_copy(up_hbm.at[0, span], up_w.at[i], wsems.at[i, 1]),
        )

    @pl.when(j == 0)
    def _():
        for copy in fetch_pieces(pieces, buffer, sems, parts):
            copy.start()
        for i in range(2):
            for copy in weights(i):
                copy.start()

    @pl.when(j < steps)
    def _():
        await_pieces(pieces, buffer, sems, parts, j)
        part = dot(buffer[j], down_ref[...], NT)

        @pl.when(j == 0)
        def _():
            acc[...] = part

        @pl.when(j > 0)
        def _():
            acc[...] += part

    @pl.when(j == steps - 1)
    def _():
        hidden = acc[...]
        gg_ref[...] = (hidden * a_ref[...].astype(F32)).astype(BF16)
        ug_ref[...] = (hidden * b_ref[...].astype(F32)).astype(BF16)

    for i, out_ref in enumerate((out_a, out_b)):

        @pl.when(j == steps + i)
        def _():
            for copy in weights(i):
                copy.wait()
            out_ref[...] = (
                dot(gg_ref[...], gate_w[i], NT) + dot(ug_ref[...], up_w[i], NT)
            ).astype(BF16)


def hidden_and_far(blocks, pieces, down, gate, up, a, b, steps, parts):
    rows = pieces[0].shape[0] * parts
    depth = pieces[0].shape[1]
    hidden = gate.shape[2]
    whole = pl.BlockSpec((rows, hidden), lambda j, blk: (0, 0))
    out = pl.BlockSpec((rows, depth), lambda j, blk: (0, 0))
    return pl.pallas_call(
        functools.partial(hidden_kernel, steps, parts),
        name="hidden_far",
        grid_spec=pltpu.PrefetchScalarGridSpec(
            num_scalar_prefetch=1,
            grid=(steps + 2,),
            in_specs=[ANY] * len(pieces)
            + [
                pl.BlockSpec(
                    (None, hidden, depth), lambda j, blk: (0, 0, blk[jnp.minimum(j, steps - 1)])
                ),
                ANY,
                ANY,
                whole,
                whole,
            ],
            out_specs=[whole, whole, out, out],
            scratch_shapes=[
                pltpu.VMEM((steps, rows, depth), BF16),
                pltpu.VMEM((rows, hidden), F32),
                pltpu.VMEM((2, depth, hidden), BF16),
                pltpu.VMEM((2, depth, hidden), BF16),
                pltpu.SemaphoreType.DMA((steps, parts)),
                pltpu.SemaphoreType.DMA((2, 2)),
            ],
        ),
        out_shape=[jax.ShapeDtypeStruct((rows, hidden), BF16)] * 2
        + [jax.ShapeDtypeStruct((rows, depth), BF16)] * 2,
        cost_estimate=cost(4 * rows * depth * steps * hidden, 4 * depth * steps * hidden),
    )(blocks, *pieces, down, gate, up, a, b)


def near_kernel(blk_ref, gg_ref, ug_ref, gate_ref, up_ref, out_a, out_b):
    j = pl.program_id(0)
    value = (dot(gg_ref[...], gate_ref[...], NT) + dot(ug_ref[...], up_ref[...], NT)).astype(BF16)

    @pl.when(j == 0)
    def _():
        out_a[...] = value

    @pl.when(j == 1)
    def _():
        out_b[...] = value


def near_half(blocks, gg, ug, gate, up, depth):
    rows, hidden = gg.shape
    whole = pl.BlockSpec((rows, hidden), lambda j, blk: (0, 0))
    weight = pl.BlockSpec((None, depth, hidden), lambda j, blk: (0, blk[j], 0))
    out = pl.BlockSpec((rows, depth), lambda j, blk: (0, 0))
    return pl.pallas_call(
        near_kernel,
        name="near_half",
        grid_spec=pltpu.PrefetchScalarGridSpec(
            num_scalar_prefetch=1,
            grid=(2,),
            in_specs=[whole, whole, weight, weight],
            out_specs=[out, out],
        ),
        out_shape=[jax.ShapeDtypeStruct((rows, depth), BF16)] * 2,
        cost_estimate=cost(8 * rows * depth * hidden, 8 * depth * hidden),
    )(blocks, gg, ug, gate, up)


def combine_kernel(w_hi_ref, w_lo_ref, *refs):
    pieces, out_ref, table = refs[:-2], refs[-2], refs[-1]
    cap = pieces[0].shape[0]
    for i, ref in enumerate(pieces):
        table[i * cap : (i + 1) * cap] = ref[...]
    rows = table[...]
    out_ref[...] = (dot(w_hi_ref[...], rows) + dot(w_lo_ref[...], rows)).astype(BF16)


def combine(w_hi, w_lo, pieces):
    tokens, rows = w_hi.shape
    width = pieces[0].shape[1]
    return pl.pallas_call(
        combine_kernel,
        name="combine",
        out_shape=jax.ShapeDtypeStruct((tokens, width), BF16),
        scratch_shapes=[pltpu.VMEM((rows, width), BF16)],
        cost_estimate=cost(4 * tokens * rows * width, 4 * rows * width),
    )(w_hi, w_lo, *pieces)


def cumulative(decay_ref):
    length = decay_ref.shape[1]
    t = lax.broadcasted_iota(jnp.int32, (length, length), 0)
    r = lax.broadcasted_iota(jnp.int32, (length, length), 1)
    lower = (r <= t).astype(F32)
    columns = dot(lower, decay_ref[...], NT, HIGHEST)
    rows = dot(decay_ref[...], lower, NT, HIGHEST)
    return columns, rows, r <= t


def summary_kernel(group, width, odd_ref, q_ref, k_ref, v_ref, g_ref, decay_ref, out_ref):
    odd = odd_ref[0]
    columns, _, _ = cumulative(decay_ref)
    length = columns.shape[0]
    total = columns[length - 1 : length, :]
    front = jnp.exp(columns)
    tail = jnp.exp(total - columns)
    whole = jnp.exp(total)
    for side in range(2):
        where = side ^ odd
        tile = jnp.zeros((16, width), F32)
        row = lax.broadcasted_iota(jnp.int32, (16, width), 0)
        for i in range(group):
            h = side * group + i
            span = slice(h * width, (h + 1) * width)
            key = (k_ref[:, span].astype(F32) * tail[:, h : h + 1]).astype(BF16)
            query = (q_ref[:, span].astype(F32) * front[:, h : h + 1]).astype(BF16)
            out_ref[where, i * width : (i + 1) * width] = dot(key, v_ref[:, span], TN).astype(BF16)
            out_ref[where, (group + i) * width : (group + i + 1) * width] = dot(
                query, g_ref[:, span], TN
            ).astype(BF16)
            decay = whole[:, h : h + 1]
            high = decay.astype(BF16).astype(F32)
            tile = jnp.where(row == i, high, tile)
            tile = jnp.where(row == group + i, decay - high, tile)
        out_ref[where, 2 * group * width :] = tile.astype(BF16)


def summaries(odd, q, k, v, g, decay, group, width):
    return pl.pallas_call(
        functools.partial(summary_kernel, group, width),
        name="summaries",
        out_shape=jax.ShapeDtypeStruct((2, 2 * group * width + 16, width), BF16),
        in_specs=[SMEM] + [pl.BlockSpec(memory_space=pltpu.VMEM)] * 5,
        cost_estimate=cost(8 * group * width**3, 16 * group * width * width),
    )(odd, q, k, v, g, decay)


def decay_rows(ref, group, base):
    tile = ref[base : base + 16].astype(F32)
    return [tile[i : i + 1] + tile[group + i : group + i + 1] for i in range(group)]


def pair_kernel(group, width, steps, where_ref, mine_ref, other_ref, *out_refs):
    odd, at = where_ref[0], where_ref[1]
    base = 2 * group * width
    even = odd == 0
    mine_decay = decay_rows(mine_ref, group, base)
    other_decay = decay_rows(other_ref, group, base)
    row = lax.broadcasted_iota(jnp.int32, (16, width), 0)
    tile = jnp.zeros((16, width), F32)
    for i in range(group):
        kv_span = slice(i * width, (i + 1) * width)
        qo_span = slice((group + i) * width, (group + i + 1) * width)
        kv_mine, kv_other = mine_ref[kv_span].astype(F32), other_ref[kv_span].astype(F32)
        qo_mine, qo_other = mine_ref[qo_span].astype(F32), other_ref[qo_span].astype(F32)
        d_mine, d_other = mine_decay[i], other_decay[i]
        forward = jnp.where(even, d_other * kv_mine + kv_other, d_mine * kv_other + kv_mine)
        backward = jnp.where(even, qo_mine + d_mine * qo_other, qo_other + d_other * qo_mine)
        forward, backward = forward.astype(BF16), backward.astype(BF16)
        for m in range(1, steps):
            out_refs[m - 1][kv_span] = jnp.where((at ^ m) > at, forward, backward)
        both = d_mine * d_other
        high = both.astype(BF16).astype(F32)
        tile = jnp.where(row == i, high, tile)
        tile = jnp.where(row == group + i, both - high, tile)
    for m in range(1, steps):
        out_refs[m - 1][group * width :] = tile.astype(BF16)


def pair_totals(where, mine, other, group, width, steps):
    shape = jax.ShapeDtypeStruct((group * width + 16, width), BF16)
    return pl.pallas_call(
        functools.partial(pair_kernel, group, width, steps),
        name="pair_totals",
        out_shape=[shape] * (steps - 1),
        in_specs=[SMEM] + [pl.BlockSpec(memory_space=pltpu.VMEM)] * 2,
        cost_estimate=cost(8 * group * width**2, 16 * group * width * width),
    )(where, mine, other)


def state_kernel(group, width, steps, where_ref, mine_ref, other_ref, prefix_ref, *refs):
    received, (own_ref, give_ref) = refs[: steps - 1], refs[steps - 1 :]
    odd, at = where_ref[0], where_ref[1]
    even = odd == 0
    mine_decay = decay_rows(mine_ref, group, 2 * group * width)
    other_decay = decay_rows(other_ref, group, 2 * group * width)
    pair_decay = [decay_rows(ref, group, group * width) for ref in received]
    for i in range(group):
        kv_span = slice(i * width, (i + 1) * width)
        qo_span = slice((group + i) * width, (group + i + 1) * width)
        through = jnp.ones((1, width), F32)
        for n in range(1, steps):
            through = through * jnp.where((at ^ n) < at, pair_decay[n - 1][i], 1.0)
        state = through * prefix_ref[odd * group + i]
        grad = jnp.zeros((width, width), F32)
        for m in range(1, steps):
            there = at ^ m
            earlier = there < at
            low, high = jnp.minimum(there, at), jnp.maximum(there, at)
            factor = jnp.ones((1, width), F32)
            for n in range(1, steps):
                between = ((at ^ n) > low) & ((at ^ n) < high)
                factor = factor * jnp.where(between, pair_decay[n - 1][i], 1.0)
            term = factor * received[m - 1][kv_span].astype(F32)
            state = state + jnp.where(earlier, term, 0.0)
            grad = grad + jnp.where(earlier, 0.0, term)
        kv_mine, kv_other = mine_ref[kv_span].astype(F32), other_ref[kv_span].astype(F32)
        qo_mine, qo_other = mine_ref[qo_span].astype(F32), other_ref[qo_span].astype(F32)
        d_mine, d_other = mine_decay[i], other_decay[i]
        state_odd = jnp.where(even, d_mine * state + kv_mine, d_other * state + kv_other)
        grad_even = jnp.where(even, d_other * grad + qo_other, d_mine * grad + qo_mine)
        own_ref[kv_span] = jnp.where(even, state, state_odd).astype(BF16)
        give_ref[kv_span] = jnp.where(even, state_odd, state).astype(BF16)
        own_ref[qo_span] = jnp.where(even, grad_even, grad).astype(BF16)
        give_ref[qo_span] = jnp.where(even, grad, grad_even).astype(BF16)


def states(where, mine, other, prefix, received, group, width, steps):
    shape = jax.ShapeDtypeStruct((2 * group * width, width), BF16)
    return pl.pallas_call(
        functools.partial(state_kernel, group, width, steps),
        name="states",
        out_shape=[shape, shape],
        in_specs=[SMEM] + [pl.BlockSpec(memory_space=pltpu.VMEM)] * (3 + len(received)),
        cost_estimate=cost(16 * group * width**2, 32 * group * width * width),
    )(where, mine, other, prefix, *received)


def attention_kernel(group, width, *refs):
    odd_ref, q_ref, k_ref, v_ref, g_ref, decay_ref, own_ref, got_ref, dq_ref, dk_ref, dv_ref = refs
    odd = odd_ref[0]
    columns, rows, causal = cumulative(decay_ref)
    length = columns.shape[0]
    total = columns[length - 1 : length, :]
    front = jnp.exp(columns)
    tail = jnp.exp(total - columns)
    for h in range(2 * group):
        span = slice(h * width, (h + 1) * width)
        i = h % group
        kv_span = slice(i * width, (i + 1) * width)
        qo_span = slice((group + i) * width, (group + i + 1) * width)
        mine = (h // group) == odd
        state = jnp.where(mine, own_ref[kv_span].astype(F32), got_ref[kv_span].astype(F32))
        grad = jnp.where(mine, own_ref[qo_span].astype(F32), got_ref[qo_span].astype(F32))
        state, grad = state.astype(BF16), grad.astype(BF16)
        q, k, v, g = q_ref[:, span], k_ref[:, span], v_ref[:, span], g_ref[:, span]
        spread = columns[:, h : h + 1] - rows[h : h + 1, :]
        within = jnp.where(causal, jnp.exp(jnp.where(causal, spread, 0.0)), 0.0)
        value_scores = (dot(g, v, NT) * within).astype(BF16)
        key_scores = (dot(q, k, NT) * within).astype(BF16)
        f, e = front[:, h : h + 1], tail[:, h : h + 1]
        dq_ref[:, span] = (dot(value_scores, k) + f * dot(g, state, NT)).astype(BF16)
        dk_ref[:, span] = (dot(value_scores, q, TN) + e * dot(v, grad, NT)).astype(BF16)
        dv_ref[:, span] = (dot(key_scores, g, TN) + e * dot(k, grad)).astype(BF16)


def attention(odd, q, k, v, g, decay, own, got, group, width):
    return pl.pallas_call(
        functools.partial(attention_kernel, group, width),
        name="attention",
        out_shape=[jax.ShapeDtypeStruct(q.shape, BF16)] * 3,
        in_specs=[SMEM] + [pl.BlockSpec(memory_space=pltpu.VMEM)] * 7,
        cost_estimate=cost(32 * group * width**3, 32 * group * width * width),
    )(odd, q, k, v, g, decay, own, got)


def shards(
    queries,
    keys,
    values,
    out_grad,
    log_decay,
    prefix_state,
    moe_input,
    moe_grad,
    expert_gate,
    expert_up,
    expert_down,
    expert_ids,
    route_probs,
):
    heads, length = log_decay.shape
    width = prefix_state.shape[1]
    group = heads // 2
    n = lax.axis_size("ctx")
    steps = n // 2
    cap = 4 * length // n
    depth = moe_input.shape[1]
    ctx = lax.axis_index("ctx").astype(jnp.int32)
    head = lax.axis_index("head").astype(jnp.int32)
    odd = jnp.reshape(ctx & 1, (1,))
    where = jnp.stack([ctx & 1, ctx >> 1])

    w_hi, w_lo, in_even, in_odd, grad_even, grad_odd = route(
        jnp.reshape(ctx, (1,)), expert_ids, route_probs, moe_input, moe_grad, n, cap
    )

    def gathered(even, odd_rows):
        other = xor_permute(odd_rows, "ctx", 1)
        chunks = []
        for m in range(steps):
            both = jnp.concatenate([even[m], other[m]], axis=0)
            chunks.append(both if m == 0 else xor_permute(both, "ctx", 2 * m))
        lower = jnp.concatenate(chunks[: steps // 2], axis=0)
        upper = jnp.concatenate(chunks[steps // 2 :], axis=0)
        own = [lower, upper]
        far = [xor_permute(part, "head", 2) for part in own]
        near_own = [xor_permute(part, "head", 1) for part in own]
        near_far = [xor_permute(part, "head", 1) for part in far]
        return own + far + near_own + near_far

    def block_list(offsets):
        return jnp.stack([head ^ o for o in offsets])

    in_pieces = gathered(in_even, in_odd)
    grad_pieces = gathered(grad_even, grad_odd)

    summary = summaries(odd, queries, keys, values, out_grad, log_decay, group, width)
    mine, theirs = summary[0], summary[1]
    other = xor_permute(theirs, "ctx", 1)
    outgoing = pair_totals(where, mine, other, group, width, steps)
    received = [xor_permute(out, "ctx", 2 * (m + 1)) for m, out in enumerate(outgoing)]
    own_state, give_state = states(
        where, mine, other, prefix_state, received, group, width, steps
    )
    got_state = xor_permute(give_state, "ctx", 1)

    a, b = gate_up(block_list((0, 2, 1, 3)), in_pieces, expert_gate, expert_up, 4, 2)
    gg, ug, out3, out2 = hidden_and_far(
        block_list((0, 2, 1, 3, 3, 2)),
        grad_pieces,
        expert_down,
        expert_gate,
        expert_up,
        a,
        b,
        4,
        2,
    )
    rows = out3.shape[0]
    from3 = xor_permute(out3, "head", 1)
    halves = ((rows // 2, rows), (0, rows // 2))
    far_sums = [
        (out2[lo:hi].astype(F32) + from3[lo:hi].astype(F32)).astype(BF16) for lo, hi in halves
    ]
    from_far = [xor_permute(part, "head", 2) for part in far_sums]
    out1, out0 = near_half(block_list((1, 0)), gg, ug, expert_gate, expert_up, depth)
    from1 = xor_permute(out1, "head", 1)
    table = {}
    for (lo, hi), got in zip(halves, from_far):
        for r in range(lo // cap, hi // cap):
            s, e = r * cap, (r + 1) * cap
            total = (
                out0[s:e].astype(F32)
                + from1[s:e].astype(F32)
                + got[s - lo : e - lo].astype(F32)
            ).astype(BF16)
            table[r] = total if r == 0 else xor_permute(total, "ctx", r)
    moe_input_grad = combine(w_hi, w_lo, [table[r] for r in range(n)])

    query_grad, key_grad, value_grad = attention(
        odd, queries, keys, values, out_grad, log_decay, own_state, got_state, group, width
    )
    return (query_grad, key_grad, value_grad, moe_input_grad)


def solution(mesh):
    in_specs = (
        P("ctx", "head"),
        P("ctx", "head"),
        P("ctx", "head"),
        P("ctx", "head"),
        P("head", "ctx"),
        P("head", None, None),
        P("ctx", "head"),
        P("ctx", "head"),
        P("ctx", None, "head"),
        P("ctx", None, "head"),
        P("ctx", "head", None),
        P("ctx", None),
        P("ctx", None),
    )
    out_specs = (P("ctx", "head"), P("ctx", "head"), P("ctx", "head"), P("ctx", "head"))
    return jax.shard_map(shards, mesh=mesh, in_specs=in_specs, out_specs=out_specs, check_vma=False)
```
